32 devices in a mesh: dp: 4 (over x, core), head: 8 (over z, y).
Axes of the slice: x: 2, y: 2, z: 4, core: 2. Of those that a mesh axis runs over, the one named last changes fastest.
Arguments:
- query_nope: bfloat16 [2, 512, 2048], P(None, ('dp', 'head')), may hold values from -12 to 12
- query_rope: bfloat16 [2, 512, 1024], P(None, ('dp', 'head')), may hold values from -640 to 640
- key_up: bfloat16 [2, 16, 128, 512], P(None, 'dp'), may hold values from -0.5 to 0.5
- value_up: bfloat16 [2, 16, 512, 128], P(None, 'dp'), may hold values from -0.25 to 0.25
- pool_latent: bfloat16 [2, 8, 128, 512], P(None, 'head'), may hold values from -6 to 6
- pool_rope: bfloat16 [2, 8, 64, 128], P(None, 'head'), may hold values from -8 to 8
- block_table: int32 [2, 6], replicated, may hold values from 0 to 7, as said below
- suffix_latent: bfloat16 [2, 512, 128, 512], P(None, ('dp', 'head')), may hold values from -8 to 8
- suffix_rope: bfloat16 [2, 512, 64, 128], P(None, ('dp', 'head')), may hold values from -8 to 8
- lengths: int32 [512], P(('dp', 'head')), may hold values from 1 to 128, as said below
Outputs:
- attention: bfloat16 [2, 512, 2048], P(None, ('dp', 'head'))
The draws below stay inside these ranges and needn't reach their ends.
Inputs may be any that keep to these rules, and one draw needn't show every extreme that they name: `block_table`: each row names 6 different slots. `lengths`: among the 16 sequences of every device at least one has length 128.
All inputs are finite; a program needn't handle non-finite values.
Results may differ from the reference program's by a relative error of at most 0.0087.
Values may be sent and summed in bfloat16 or wider, within the bound.
A program may use at most 128 MiB of HBM per device.

```python
import jax
import jax.numpy as jnp
from jax import lax

HEADS = 16
RANK = 512
NOPE = 128
ROPE = 64
VDIM = 128
LAYERS = 2
SEQ_DEV = 16
SUF = 128
BLK = 128
POOL = 8
NBLK = 6
PREFIX = 768
SEQS = 512


def slot_table(key):
    layer_keys = jax.random.split(jax.random.fold_in(key, 7), LAYERS)
    chosen = jax.vmap(lambda item_key: jax.random.permutation(item_key, POOL)[:NBLK])(layer_keys)
    return chosen.astype(jnp.int32)


def rope_base(key):
    noise = jax.random.normal(jax.random.fold_in(key, 21), (LAYERS, POOL, ROPE, BLK), jnp.float32)
    return jnp.clip(noise, -4.0, 4.0)


def unit_keys(key):
    base = rope_base(key)
    return base


def draw_block_table(key, part):
    return slot_table(key)


def draw_lengths(key, part):
    first_key, second_key = jax.random.split(jax.random.fold_in(key, 41))
    drawn = jax.random.randint(first_key, (SEQS,), 1, SUF + 1)
    devices_count = SEQS // SEQ_DEV
    full_pick = jax.random.randint(second_key, (devices_count,), 0, SEQ_DEV)
    positions = jnp.arange(devices_count) * SEQ_DEV + full_pick
    return drawn.at[positions].set(SUF).astype(jnp.int32)


def draw_pool_rope(key, part):
    base = unit_keys(key)
    return base.astype(jnp.bfloat16)


def draw_query_rope(key, part):
    noise = jax.random.normal(jax.random.fold_in(key, 23), (LAYERS, SEQS, HEADS * ROPE), jnp.float32)
    values = jnp.clip(2.0 * noise, -12.0, 12.0)
    return values.astype(jnp.bfloat16)


def draw_query_nope(key, part):
    noise = jax.random.normal(jax.random.fold_in(key, 25), (LAYERS, SEQS, HEADS * NOPE), jnp.float32)
    values = jnp.clip(2.0 * noise, -12.0, 12.0)
    return values.astype(jnp.bfloat16)


def levels(key, shape, shards, smallest, top_value):
    factor_of = 1.0
    for axis_at, parts in shards:
        steps = jax.random.uniform(jax.random.fold_in(jax.random.fold_in(key, 6), axis_at), (parts,), jnp.float32, smallest / len(shards), top_value / len(shards))
        factor_of = factor_of * jnp.repeat(jnp.exp(steps), shape[axis_at] // parts).reshape((-1,) + (1,) * (len(shape) - 1 - axis_at))
    return factor_of


def centred(stream_key, dims, scale, reach, shards=(), kind=jnp.bfloat16):
    loudness = levels(stream_key, dims, shards, -0.22, 0.18) if shards else 1.0
    result = jax.random.normal(stream_key, dims, jnp.float32) * scale * loudness
    return jnp.minimum(jnp.maximum(result, -reach), reach).astype(kind)


def setup_inputs(seed: int = 0) -> dict:
    key_list = jax.random.split(jax.random.key(seed), 11)
    return {
        "query_nope": draw_query_nope(jax.random.fold_in(key_list[10], 71), 0),
        "query_rope": draw_query_rope(jax.random.fold_in(key_list[10], 71), 0),
        "key_up": centred(key_list[2], (LAYERS, HEADS, NOPE, RANK), NOPE ** -0.5, 0.5, ((1, 4),)),
        "value_up": centred(key_list[3], (LAYERS, HEADS, RANK, VDIM), RANK ** -0.5, 0.25, ((1, 4),)),
        "pool_latent": centred(key_list[4], (LAYERS, POOL, BLK, RANK), 1.0, 6.0, ((1, 8),)),
        "pool_rope": draw_pool_rope(jax.random.fold_in(key_list[10], 71), 0),
        "block_table": draw_block_table(jax.random.fold_in(key_list[10], 71), 0),
        "suffix_latent": centred(key_list[7], (LAYERS, SEQS, SUF, RANK), 1.25, 8.0, ((1, 32),)),
        "suffix_rope": centred(key_list[8], (LAYERS, SEQS, ROPE, SUF), 1.25, 8.0, ((1, 32),)),
        "lengths": draw_lengths(jax.random.fold_in(key_list[10], 71), 0),
    }


def rounded(values):
    return lax.optimization_barrier(values.astype(jnp.bfloat16)).astype(jnp.float32)


def reference(query_nope, query_rope, key_up, value_up, pool_latent, pool_rope, block_table, suffix_latent, suffix_rope, lengths):
    scale = (NOPE + ROPE) ** -0.5
    groups = SEQS // SEQ_DEV
    results = []
    for layer_index in range(LAYERS):
        chosen = block_table[layer_index].astype(jnp.int32)
        prefix_latent = pool_latent[layer_index][chosen].reshape(PREFIX, RANK).astype(jnp.float32)
        prefix_rope = jnp.transpose(pool_rope[layer_index][chosen], (1, 0, 2)).reshape(ROPE, PREFIX).astype(jnp.float32)
        key_weight = key_up[layer_index].astype(jnp.float32)
        value_weight = value_up[layer_index].astype(jnp.float32)

        def one_block(items):
            query_heads, query_rotary, own_latent, own_rope, seq_lengths = items
            query_heads = query_heads.astype(jnp.float32)
            query_rotary = query_rotary.astype(jnp.float32)
            own_latent = own_latent.astype(jnp.float32)
            own_rope = own_rope.astype(jnp.float32)
            q_latent = rounded(jnp.einsum('bhd,hdc->bhc', query_heads, key_weight))
            prefix_scores = (jnp.einsum('bhc,tc->bht', q_latent, prefix_latent) + jnp.einsum('bhr,rt->bht', query_rotary, prefix_rope)) * scale
            suffix_scores = (jnp.einsum('bhc,btc->bht', q_latent, own_latent) + jnp.einsum('bhr,brt->bht', query_rotary, own_rope)) * scale
            live_mask = (jnp.arange(SUF)[None, :] < seq_lengths[:, None])[:, None, :]
            row_max = jnp.maximum(jnp.max(prefix_scores, axis=-1), jnp.max(jnp.where(live_mask, suffix_scores, -jnp.inf), axis=-1))
            prefix_exp = jnp.exp(prefix_scores - row_max[..., None])
            suffix_exp = jnp.where(live_mask, jnp.exp(suffix_scores - row_max[..., None]), 0.0)
            row_total = jnp.sum(prefix_exp, axis=-1) + jnp.sum(suffix_exp, axis=-1)
            gathered = jnp.einsum('bht,tc->bhc', rounded(prefix_exp), prefix_latent) + jnp.einsum('bht,btc->bhc', rounded(suffix_exp), own_latent)
            latent_out = rounded(gathered / row_total[..., None])
            expanded = jnp.einsum('bhc,hcv->bhv', latent_out, value_weight)
            return expanded.astype(jnp.bfloat16).reshape(SEQ_DEV, HEADS * VDIM)

        items = (
            query_nope[layer_index].reshape(groups, SEQ_DEV, HEADS, NOPE),
            query_rope[layer_index].reshape(groups, SEQ_DEV, HEADS, ROPE),
            suffix_latent[layer_index].reshape(groups, SEQ_DEV, SUF, RANK),
            suffix_rope[layer_index].reshape(groups, SEQ_DEV, ROPE, SUF),
            lengths.reshape(groups, SEQ_DEV),
        )
        blocks_out = lax.map(one_block, items)
        results.append(blocks_out.reshape(SEQS, HEADS * VDIM))
    return jnp.stack(results)
```

```python
import functools

import jax
import jax.numpy as jnp
from jax import lax
from jax.experimental import pallas as pl
from jax.experimental.pallas import tpu as pltpu
from jax.sharding import PartitionSpec as P

HEADS = 16
NOPE = 128
ROPE = 64
VDIM = 128
SCALE = (NOPE + ROPE) ** (-0.5)
MESH = pl.DeviceIdType.MESH
F32 = jnp.float32
BF16 = jnp.bfloat16
NT = (((1,), (1,)), ((), ()))


def dot(a, b):
    return jnp.dot(a, b, preferred_element_type=F32)


def dot_nt(a, b):
    return lax.dot_general(a, b, NT, preferred_element_type=F32)


def kernel(dims, *refs):
    (layers, seqs, groups, heads_dev, rank, blk, suf, per, ring, nblk, chunk) = dims
    it = iter(refs)

    def take(count):
        return [next(it) for _ in range(count)]

    qn, qr, ku, vu, pool_lat, pool_rope, table, suf_lat, suf_rope, lengths = take(10)
    (out,) = take(1)
    qr_v, ku_v, vu_v, sl_v, sr_v = take(5)
    plat = take(layers)
    prope = take(layers)
    hq, scr, qls, qlat, qrf, qrot, m_ref, l_ref, acc, s_ref, kbuf, rbuf, los, lr, hvs = take(15)
    (
        loc_sem, pown_sem, own_sem,
        q_ss, q_rs, ql_ss, ql_rs, lo_ss, lo_rs, hv_ss, hv_rs,
        z_ss, z_rs, y_ss, y_rs, c_ss, c_rs,
    ) = take(17)

    dp = lax.axis_index("dp")
    hd = lax.axis_index("head")
    core = lax.rem(dp, 2)
    partner = dp + 1 - 2 * core
    za, yb = hd // 2, lax.rem(hd, 2)
    outer = ring // 2
    wide = heads_dev * NOPE
    rows_g = seqs * heads_dev
    rows = groups * rows_g
    quad = 16 // heads_dev
    nquads = seqs // quad

    local = []

    def fetch(src, dst, sem):
        cp = pltpu.make_async_copy(src, dst, sem)
        cp.start()
        return cp

    def own_q(l):
        return pltpu.make_async_copy(
            qn.at[l, :, pl.ds(pl.multiple_of(dp * wide, 128), wide)], hq.at[l, dp], own_sem.at[0, l]
        )

    for l in range(layers):
        own_q(l).start()
    c_ku = [fetch(ku.at[l], ku_v.at[l], loc_sem.at[0, l]) for l in range(layers)]
    c_qr = fetch(qr, qr_v, loc_sem.at[1, 0])
    c_sl = [fetch(suf_lat.at[l], sl_v.at[l], loc_sem.at[2, l]) for l in range(layers)]
    c_sr = [fetch(suf_rope.at[l], sr_v.at[l], loc_sem.at[3, l]) for l in range(layers)]
    c_po = []
    for l in range(layers):
        mine = pl.ds(hd * per, per)
        c_po.append(fetch(pool_lat.at[l], plat[l].at[mine], pown_sem.at[0, l]))
        c_po.append(fetch(pool_rope.at[l], prope[l].at[mine], pown_sem.at[1, l]))
    c_vu = [fetch(vu.at[l], vu_v.at[l], loc_sem.at[4, l]) for l in range(layers)]

    barrier = pltpu.get_barrier_semaphore()

    def greet(d, h):
        pl.semaphore_signal(barrier, inc=1, device_id=(d, h), device_id_type=MESH)

    for i in range(1, groups):
        greet(lax.rem(dp + i, groups), hd)
    for_z = lambda i: lax.rem(za + i, outer)

    def greet_z(i, carry):
        greet(dp, for_z(i) * 2 + yb)
        return carry

    lax.fori_loop(1, outer, greet_z, 0)
    greet(dp, za * 2 + 1 - yb)
    pl.semaphore_wait(barrier, (groups - 1) + (outer - 1) + 1)

    def remote(src, dst, ss, rs, d, h):
        return pltpu.make_async_remote_copy(
            src_ref=src, dst_ref=dst, send_sem=ss, recv_sem=rs, device_id=(d, h), device_id_type=MESH
        )

    def peer(i):
        return lax.rem(dp + i, groups)

    def send_q(l, i):
        j = peer(i)
        return remote(
            qn.at[l, :, pl.ds(pl.multiple_of(j * wide, 128), wide)], hq.at[l, dp],
            q_ss.at[l, j], q_rs.at[l, dp], j, hd,
        )

    def recv_q(l, i):
        j = peer(i)
        return remote(hq.at[l, j], hq.at[l, j], q_ss.at[l, j], q_rs.at[l, j], j, hd)

    def pair(sends, buf, ss, rs):
        def send(l, i):
            j = peer(i)
            return remote(sends.at[l, j], buf.at[l, dp], ss.at[l, j], rs.at[l, dp], j, hd)

        def recv(l, i):
            j = peer(i)
            return remote(sends.at[l, j], buf.at[l, j], ss.at[l, j], rs.at[l, j], j, hd)

        return send, recv

    send_ql, recv_ql = pair(qls, qlat, ql_ss, ql_rs)
    send_lo, recv_lo = pair(los, lr, lo_ss, lo_rs)

    def cols(j):
        return pl.ds(pl.multiple_of(j * heads_dev * VDIM, 128), heads_dev * VDIM)

    def send_hv(l, i):
        j = peer(i)
        return remote(hvs.at[l, j], out.at[l, :, cols(dp)], hv_ss.at[l, j], hv_rs.at[l, dp], j, hd)

    def recv_hv(l, i):
        j = peer(i)
        return remote(hvs.at[l, j], out.at[l, :, cols(j)], hv_ss.at[l, j], hv_rs.at[l, j], j, hd)

    def half(kind, c):
        size = (blk if kind == 0 else ROPE) // 2
        return pl.ds(pl.multiple_of(c * size, 16), size)

    def pool_at(l, kind, slot, c):
        buf = (plat if kind == 0 else prope)[l]
        return buf.at[pl.ds(slot * per, per), half(kind, c)]

    def own_piece(l, kind):
        return (pool_lat if kind == 0 else pool_rope).at[l, :, half(kind, core)]

    def send_z(l, kind, i):
        to = for_z(i)
        return remote(
            own_piece(l, kind), pool_at(l, kind, hd, core),
            z_ss.at[l, kind, to], z_rs.at[l, kind, za], dp, to * 2 + yb,
        )

    def recv_z(l, kind, i):
        frm = for_z(i)
        return remote(
            own_piece(l, kind), pool_at(l, kind, frm * 2 + yb, core),
            z_ss.at[l, kind, frm], z_rs.at[l, kind, frm], dp, frm * 2 + yb,
        )

    def send_y(l, kind, a, src):
        return remote(
            src, pool_at(l, kind, a * 2 + yb, core),
            y_ss.at[l, kind, a], y_rs.at[l, kind, a], dp, za * 2 + 1 - yb,
        )

    def recv_y(l, kind, a):
        return remote(
            own_piece(l, kind), pool_at(l, kind, a * 2 + 1 - yb, core),
            y_ss.at[l, kind, a], y_rs.at[l, kind, a], dp, za * 2 + 1 - yb,
        )

    def send_c(l, kind, slot):
        piece = pool_at(l, kind, slot, core)
        return remote(piece, piece, c_ss.at[l, kind, slot], c_rs.at[l, kind, slot], partner, hd)

    def recv_c(l, kind, slot):
        piece = pool_at(l, kind, slot, 1 - core)
        return remote(piece, piece, c_ss.at[l, kind, slot], c_rs.at[l, kind, slot], partner, hd)

    def loop(low, high, body):
        def step(i, carry):
            body(i)
            return carry

        lax.fori_loop(low, high, step, 0)

    for l in range(layers):
        for i in range(1, groups):
            send_q(l, i).start()
    for l in range(layers):
        for kind in range(2):
            send_y(l, kind, za, own_piece(l, kind)).start()

        def first(i):
            for kind in range(2):
                send_z(l, kind, i).start()

        loop(1, outer, first)

    def forward_z(l):
        def body(i):
            for kind in range(2):
                recv_z(l, kind, i).wait_recv()
                a = for_z(i)
                send_y(l, kind, a, pool_at(l, kind, a * 2 + yb, core)).start()
                send_c(l, kind, a * 2 + yb).start()

        loop(1, outer, body)

    def forward_y(l):
        def body(i):
            for kind in range(2):
                a = for_z(i)
                recv_y(l, kind, a).wait_recv()
                send_c(l, kind, a * 2 + 1 - yb).start()

        loop(0, outer, body)

    def others(body):
        loop(1, ring, lambda i: body(lax.rem(hd + i, ring)))

    def gather_c(l):
        def body(slot):
            for kind in range(2):
                recv_c(l, kind, slot).wait_recv()

        others(body)

    c_qr.wait()
    for l in range(layers):
        for g in range(groups):
            for h in range(heads_dev):
                at = (g * heads_dev + h) * ROPE
                piece = qr_v[l, :, (at // 128) * 128 : (at // 128 + 1) * 128].astype(F32)
                if at % 128:
                    piece = pltpu.roll(piece, 128 - at % 128, 1)
                qrf[pl.ds(g * rows_g + h, seqs, stride=heads_dev), :] = piece
        qrot[l] = qrf[...].astype(BF16)

    def absorb(l):
        own_q(l).wait()
        for i in range(1, groups):
            recv_q(l, i).wait_recv()
        c_ku[l].wait()
        for h in range(heads_dev):
            x = jnp.concatenate([hq[l, g, :, h * NOPE : (h + 1) * NOPE] for g in range(groups)], axis=0)
            r = dot(x, ku_v[l, h])
            for c in range(rank // 128):
                scr[c, pl.ds(h, groups * seqs, stride=heads_dev), :] = r[:, c * 128 : (c + 1) * 128]
        for g in range(groups):
            for c in range(rank // 128):
                qls[l, g, :, c * 128 : (c + 1) * 128] = scr[c, g * rows_g : (g + 1) * rows_g, :].astype(BF16)
        for i in range(1, groups):
            send_ql(l, i).start()
        qlat[l, dp] = qls[l, dp]

    def suffix(l):
        c_sl[l].wait()
        c_sr[l].wait()
        for i in range(1, groups):
            recv_ql(l, i).wait_recv()
        r_id = lax.broadcasted_iota(jnp.int32, (groups * 16, suf), 0)
        lane = lax.broadcasted_iota(jnp.int32, (groups * 16, suf), 1)
        row_seq = lax.rem(r_id // heads_dev, quad)
        for k in range(nquads):
            q = jnp.concatenate([qlat[l, g, k * 16 : (k + 1) * 16, :] for g in range(groups)], axis=0)
            qro = jnp.concatenate(
                [qrot[l, g * rows_g + k * 16 : g * rows_g + (k + 1) * 16, :] for g in range(groups)], axis=0
            )[:, :ROPE]
            keys = sl_v[l, k * quad : (k + 1) * quad].reshape(quad * suf, rank)
            turn = jnp.concatenate([sr_v[l, k * quad + u] for u in range(quad)], axis=1)
            s = (dot_nt(q, keys) + dot(qro, turn)) * SCALE
            live = jnp.concatenate(
                [(row_seq == u) & (lane < lengths[k * quad + u]) for u in range(quad)], axis=1
            )
            s = jnp.where(live, s, -jnp.inf)
            top = jnp.max(s, axis=1, keepdims=True)
            w = jnp.exp(s - top)
            tot = jnp.sum(w, axis=1, keepdims=True)
            o = dot(w.astype(BF16), keys)
            for g in range(groups):
                at = slice(g * rows_g + k * 16, g * rows_g + (k + 1) * 16)
                m_ref[l, at, :] = top[g * 16 : (g + 1) * 16]
                l_ref[l, at, :] = tot[g * 16 : (g + 1) * 16]
                acc[l, at, :] = o[g * 16 : (g + 1) * 16]

    def prefix(l):
        def some(b):
            for j in range(chunk):
                slot = table[l, b * chunk + j]
                kbuf[j * blk : (j + 1) * blk, :] = plat[l][slot]
                rbuf[:, j * blk : (j + 1) * blk] = prope[l][slot]
            q = qlat[l].reshape(rows, rank)
            s_ref[...] = (dot_nt(q, kbuf[...]) + dot(qrot[l][:, :ROPE], rbuf[...])) * SCALE
            old = m_ref[l]
            top = jnp.maximum(old, jnp.max(s_ref[...], axis=1, keepdims=True))
            w = jnp.exp(s_ref[...] - top)
            fac = jnp.exp(old - top)
            l_ref[l] = l_ref[l] * fac + jnp.sum(w, axis=1, keepdims=True)
            m_ref[l] = top
            acc[l] = acc[l] * fac + dot(w.astype(BF16), kbuf[...])

        if nblk == chunk:
            some(0)
        else:
            loop(0, nblk // chunk, some)
        res = acc[l] / l_ref[l]
        for c in range(rank // 128):
            scr[c] = res[:, c * 128 : (c + 1) * 128]
        for g in range(groups):
            for h in range(heads_dev):
                for c in range(rank // 128):
                    los[l, g, h * seqs : (h + 1) * seqs, c * 128 : (c + 1) * 128] = scr[
                        c, pl.ds(g * rows_g + h, seqs, stride=heads_dev), :
                    ].astype(BF16)
        for i in range(1, groups):
            send_lo(l, i).start()
        lr[l, dp] = los[l, dp]

    def own_out(l):
        return pltpu.make_async_copy(hvs.at[l, dp], out.at[l, :, cols(dp)], own_sem.at[1, l])

    def expand(l):
        c_vu[l].wait()
        for i in range(1, groups):
            recv_lo(l, i).wait_recv()
        for h in range(heads_dev):
            x = jnp.concatenate([lr[l, g, h * seqs : (h + 1) * seqs, :] for g in range(groups)], axis=0)
            v = dot(x, vu_v[l, h]).astype(BF16)
            for g in range(groups):
                hvs[l, g, :, h * VDIM : (h + 1) * VDIM] = v[g * seqs : (g + 1) * seqs]
        for i in range(1, groups):
            send_hv(l, i).start()
        own_out(l).start()

    for l in range(layers):
        absorb(l)
    forward_z(0)
    suffix(0)
    forward_y(0)
    for l in range(1, layers):
        forward_z(l)
        suffix(l)
        forward_y(l)
    for cp in c_po:
        cp.wait()
    for l in range(layers):
        gather_c(l)
        prefix(l)
    for l in range(layers):
        expand(l)

    for l in range(layers):
        own_out(l).wait()
        for i in range(1, groups):
            recv_hv(l, i).wait_recv()
    for l in range(layers):
        for i in range(1, groups):
            send_q(l, i).wait_send()
            send_ql(l, i).wait_send()
            send_lo(l, i).wait_send()
            send_hv(l, i).wait_send()

        def last_z(i):
            for kind in range(2):
                send_z(l, kind, i).wait_send()

        def last_y(i):
            for kind in range(2):
                send_y(l, kind, for_z(i), own_piece(l, kind)).wait_send()

        def last_c(slot):
            for kind in range(2):
                send_c(l, kind, slot).wait_send()

        loop(1, outer, last_z)
        loop(0, outer, last_y)
        others(last_c)


def on_device(mesh, *args):
    qn, qr, ku, vu, pool_lat, pool_rope, table, suf_lat, suf_rope, lengths = args
    layers, seqs, _ = qn.shape
    groups = mesh.shape["dp"]
    ring = mesh.shape["head"]
    heads_dev, rank = ku.shape[1], ku.shape[3]
    per, blk = pool_lat.shape[1], pool_lat.shape[2]
    suf = suf_lat.shape[2]
    nblk = table.shape[1]
    chunk = max(c for c in range(1, 7) if nblk % c == 0)
    rows_g = seqs * heads_dev
    rows = groups * rows_g
    slots = per * ring
    outer = ring // 2
    dims = (layers, seqs, groups, heads_dev, rank, blk, suf, per, ring, nblk, chunk)
    V = pltpu.VMEM
    D = pltpu.SemaphoreType.DMA
    scratch = [
        V(qr.shape, BF16), V(ku.shape, BF16), V(vu.shape, BF16), V(suf_lat.shape, BF16), V(suf_rope.shape, BF16),
        *[V((slots, blk, rank), BF16) for _ in range(layers)],
        *[V((slots, ROPE, blk), BF16) for _ in range(layers)],
        V((layers, groups, seqs, heads_dev * NOPE), BF16),
        V((rank // 128, rows, 128), F32),
        V((layers, groups, rows_g, rank), BF16),
        V((layers, groups, rows_g, rank), BF16),
        V((rows, 128), F32),
        V((layers, rows, 128), BF16),
        V((layers, rows, 1), F32),
        V((layers, rows, 1), F32),
        V((layers, rows, rank), F32),
        V((rows, chunk * blk), F32),
        V((chunk * blk, rank), BF16),
        V((ROPE, chunk * blk), BF16),
        V((layers, groups, rows_g, rank), BF16),
        V((layers, groups, rows_g, rank), BF16),
        V((layers, groups, seqs, heads_dev * VDIM), BF16),
        D((5, layers)), D((2, layers)), D((2, layers)),
        *[D((layers, groups)) for _ in range(8)],
        *[D((layers, 2, outer)) for _ in range(4)],
        *[D((layers, 2, ring)) for _ in range(2)],
    ]
    hbm = pl.BlockSpec(memory_space=pl.ANY)
    smem = pl.BlockSpec(memory_space=pltpu.SMEM)
    return pl.pallas_call(
        functools.partial(kernel, dims),
        out_shape=jax.ShapeDtypeStruct((layers, seqs, HEADS * VDIM), BF16),
        in_specs=[hbm] * 6 + [smem] + [hbm] * 2 + [smem],
        out_specs=hbm,
        scratch_shapes=scratch,
        compiler_params=pltpu.CompilerParams(
            collective_id=0, has_side_effects=True, vmem_limit_bytes=60 * 1024 * 1024
        ),
        name="latent_attention",
    )(*args)


def solution(mesh):
    return jax.shard_map(
        functools.partial(on_device, mesh),
        mesh=mesh,
        in_specs=(
            P(None, ("dp", "head"), None),
            P(None, ("dp", "head"), None),
            P(None, "dp", None, None),
            P(None, "dp", None, None),
            P(None, "head", None, None),
            P(None, "head", None, None),
            P(),
            P(None, ("dp", "head"), None, None),
            P(None, ("dp", "head"), None, None),
            P(("dp", "head")),
        ),
        out_specs=P(None, ("dp", "head"), None),
        check_vma=False,
    )
```

```python
import functools

import jax
import jax.numpy as jnp
from jax import lax
from jax.experimental import pallas as pl
from jax.experimental.pallas import tpu as pltpu
from jax.sharding import PartitionSpec as P

HEADS = 16
NOPE = 128
ROPE = 64
VDIM = 128
SCALE = (NOPE + ROPE) ** (-0.5)
MESH = pl.DeviceIdType.MESH
F32 = jnp.float32
BF16 = jnp.bfloat16
NT = (((1,), (1,)), ((), ()))


def dot(a, b):
    return jnp.dot(a, b, preferred_element_type=F32)


def dot_nt(a, b):
    return lax.dot_general(a, b, NT, preferred_element_type=F32)


def kernel(dims, *refs):
    (layers, seqs, groups, heads_dev, rank, blk, suf, per, ring, nblk, chunk) = dims
    it = iter(refs)

    def take(count):
        return [next(it) for _ in range(count)]

    qn, qr, ku, vu, pool_lat, pool_rope, table, suf_lat, suf_rope, lengths = take(10)
    (out,) = take(1)
    qr_v, ku_v, vu_v, sl_v, sr_v = take(5)
    plat = take(layers)
    prope = take(layers)
    hq, scr, qls, qlat, qrf, qrot, m_ref, l_ref, acc, s_ref, kbuf, rbuf, los, lr, hvs = take(15)
    (
        loc_sem, pown_sem, own_sem,
        q_ss, q_rs, ql_ss, ql_rs, lo_ss, lo_rs, hv_ss, hv_rs,
        z_ss, z_rs, y_ss, y_rs, c_ss, c_rs,
    ) = take(17)

    dp = lax.axis_index("dp")
    hd = lax.axis_index("head")
    core = lax.rem(dp, 2)
    partner = dp + 1 - 2 * core
    za, yb = hd // 2, lax.rem(hd, 2)
    outer = ring // 2
    wide = heads_dev * NOPE
    rows_g = seqs * heads_dev
    rows = groups * rows_g
    quad = 16 // heads_dev
    nquads = seqs // quad

    local = []

    def fetch(src, dst, sem):
        cp = pltpu.make_async_copy(src, dst, sem)
        cp.start()
        return cp

    def own_q(l):
        return pltpu.make_async_copy(
            qn.at[l, :, pl.ds(pl.multiple_of(dp * wide, 128), wide)], hq.at[l, dp], own_sem.at[0, l]
        )

    for l in range(layers):
        own_q(l).start()
    c_ku = [fetch(ku.at[l], ku_v.at[l], loc_sem.at[0, l]) for l in range(layers)]
    c_qr = fetch(qr, qr_v, loc_sem.at[1, 0])
    c_sl = [fetch(suf_lat.at[l], sl_v.at[l], loc_sem.at[2, l]) for l in range(layers)]
    c_sr = [fetch(suf_rope.at[l], sr_v.at[l], loc_sem.at[3, l]) for l in range(layers)]
    c_po = []
    for l in range(layers):
        mine = pl.ds(hd * per, per)
        c_po.append(fetch(pool_lat.at[l], plat[l].at[mine], pown_sem.at[0, l]))
        c_po.append(fetch(pool_rope.at[l], prope[l].at[mine], pown_sem.at[1, l]))
    c_vu = [fetch(vu.at[l], vu_v.at[l], loc_sem.at[4, l]) for l in range(layers)]

    barrier = pltpu.get_barrier_semaphore()

    def greet(d, h):
        pl.semaphore_signal(barrier, inc=1, device_id=(d, h), device_id_type=MESH)

    for i in range(1, groups):
        greet(lax.rem(dp + i, groups), hd)
    has = (za > 0, za < outer - 1)
    for side in range(2):
        pl.when(has[side])(lambda: greet(dp, (za + 2 * side - 1) * 2 + yb))
    greet(dp, za * 2 + 1 - yb)
    sides = (za + outer - 1) // outer + (2 * outer - 2 - za) // outer
    pl.semaphore_wait(barrier, groups + sides)

    def remote(src, dst, ss, rs, d, h):
        return pltpu.make_async_remote_copy(
            src_ref=src, dst_ref=dst, send_sem=ss, recv_sem=rs, device_id=(d, h), device_id_type=MESH
        )

    def peer(i):
        return lax.rem(dp + i, groups)

    def send_q(l, i):
        j = peer(i)
        return remote(
            qn.at[l, :, pl.ds(pl.multiple_of(j * wide, 128), wide)], hq.at[l, dp],
            q_ss.at[l, j], q_rs.at[l, dp], j, hd,
        )

    def recv_q(l, i):
        j = peer(i)
        return remote(hq.at[l, j], hq.at[l, j], q_ss.at[l, j], q_rs.at[l, j], j, hd)

    def pair(sends, buf, ss, rs):
        def send(l, i):
            j = peer(i)
            return remote(sends.at[l, j], buf.at[l, dp], ss.at[l, j], rs.at[l, dp], j, hd)

        def recv(l, i):
            j = peer(i)
            return remote(sends.at[l, j], buf.at[l, j], ss.at[l, j], rs.at[l, j], j, hd)

        return send, recv

    send_ql, recv_ql = pair(qls, qlat, ql_ss, ql_rs)
    send_lo, recv_lo = pair(los, lr, lo_ss, lo_rs)

    def cols(j):
        return pl.ds(pl.multiple_of(j * heads_dev * VDIM, 128), heads_dev * VDIM)

    def send_hv(l, i):
        j = peer(i)
        return remote(hvs.at[l, j], out.at[l, :, cols(dp)], hv_ss.at[l, j], hv_rs.at[l, dp], j, hd)

    def recv_hv(l, i):
        j = peer(i)
        return remote(hvs.at[l, j], out.at[l, :, cols(j)], hv_ss.at[l, j], hv_rs.at[l, j], j, hd)

    def half(kind, c):
        size = (blk if kind == 0 else ROPE) // 2
        return pl.ds(pl.multiple_of(c * size, 16), size)

    def pool_at(l, kind, slot, c):
        buf = (plat if kind == 0 else prope)[l]
        return buf.at[pl.ds(slot * per, per), half(kind, c)]

    def own_piece(l, kind):
        return (pool_lat if kind == 0 else pool_rope).at[l, :, half(kind, core)]

    def send_z(l, kind, side, a, src):
        return remote(
            src, pool_at(l, kind, a * 2 + yb, core),
            z_ss.at[l, kind, side, a], z_rs.at[l, kind, a], dp, (za + 2 * side - 1) * 2 + yb,
        )

    def recv_z(l, kind, side, a):
        return remote(
            own_piece(l, kind), pool_at(l, kind, a * 2 + yb, core),
            z_ss.at[l, kind, side, a], z_rs.at[l, kind, a], dp, (za + 2 * side - 1) * 2 + yb,
        )

    def send_y(l, kind, a, src):
        return remote(
            src, pool_at(l, kind, a * 2 + yb, core),
            y_ss.at[l, kind, a], y_rs.at[l, kind, a], dp, za * 2 + 1 - yb,
        )

    def recv_y(l, kind, a):
        return remote(
            own_piece(l, kind), pool_at(l, kind, a * 2 + 1 - yb, core),
            y_ss.at[l, kind, a], y_rs.at[l, kind, a], dp, za * 2 + 1 - yb,
        )

    def send_c(l, kind, slot):
        piece = pool_at(l, kind, slot, core)
        return remote(piece, piece, c_ss.at[l, kind, slot], c_rs.at[l, kind, slot], partner, hd)

    def recv_c(l, kind, slot):
        piece = pool_at(l, kind, slot, 1 - core)
        return remote(piece, piece, c_ss.at[l, kind, slot], c_rs.at[l, kind, slot], partner, hd)

    def loop(low, high, body):
        def step(i, carry):
            body(i)
            return carry

        lax.fori_loop(low, high, step, 0)

    for l in range(layers):
        for i in range(1, groups):
            send_q(l, i).start()
    for l in range(layers):
        for kind in range(2):
            send_y(l, kind, za, own_piece(l, kind)).start()
            for side in range(2):
                pl.when(has[side])(lambda: send_z(l, kind, side, za, own_piece(l, kind)).start())

    def at_step(i, side):
        a = za + (2 * side - 1) * i
        return a, (a >= 0 if side == 0 else a < outer)

    def span(low, high, body):
        if high - low == 1:
            body(low)
        else:
            loop(low, high, body)

    def forward_z(l, low, high):
        def body(i):
            for side in range(2):
                a, there = at_step(i, side)

                @pl.when(there)
                def _():
                    for kind in range(2):
                        recv_z(l, kind, side, a).wait_recv()
                        piece = pool_at(l, kind, a * 2 + yb, core)
                        pl.when(has[1 - side])(lambda: send_z(l, kind, 1 - side, a, piece).start())
                        send_y(l, kind, a, piece).start()
                        send_c(l, kind, a * 2 + yb).start()

        span(low, high, body)

    def pass_y(l, a):
        for kind in range(2):
            recv_y(l, kind, a).wait_recv()
            send_c(l, kind, a * 2 + 1 - yb).start()

    def forward_y(l, low, high):
        def body(i):
            for side in range(2):
                a, there = at_step(i, side)
                pl.when(there)(lambda: pass_y(l, a))

        if low == 0:
            pass_y(l, za)
        else:
            span(low, high, body)

    def others(body):
        loop(1, ring, lambda i: body(lax.rem(hd + i, ring)))

    def gather_c(l):
        def body(slot):
            for kind in range(2):
                recv_c(l, kind, slot).wait_recv()

        others(body)

    c_qr.wait()
    for l in range(layers):
        for g in range(groups):
            for h in range(heads_dev):
                at = (g * heads_dev + h) * ROPE
                piece = qr_v[l, :, (at // 128) * 128 : (at // 128 + 1) * 128].astype(F32)
                if at % 128:
                    piece = pltpu.roll(piece, 128 - at % 128, 1)
                qrf[pl.ds(g * rows_g + h, seqs, stride=heads_dev), :] = piece
        qrot[l] = qrf[...].astype(BF16)

    def absorb(l):
        own_q(l).wait()
        for i in range(1, groups):
            recv_q(l, i).wait_recv()
        c_ku[l].wait()
        for h in range(heads_dev):
            x = jnp.concatenate([hq[l, g, :, h * NOPE : (h + 1) * NOPE] for g in range(groups)], axis=0)
            r = dot(x, ku_v[l, h])
            for c in range(rank // 128):
                scr[c, pl.ds(h, groups * seqs, stride=heads_dev), :] = r[:, c * 128 : (c + 1) * 128]
        for g in range(groups):
            for c in range(rank // 128):
                qls[l, g, :, c * 128 : (c + 1) * 128] = scr[c, g * rows_g : (g + 1) * rows_g, :].astype(BF16)
        for i in range(1, groups):
            send_ql(l, i).start()
        qlat[l, dp] = qls[l, dp]

    def suffix(l):
        c_sl[l].wait()
        c_sr[l].wait()
        for i in range(1, groups):
            recv_ql(l, i).wait_recv()
        r_id = lax.broadcasted_iota(jnp.int32, (groups * 16, suf), 0)
        lane = lax.broadcasted_iota(jnp.int32, (groups * 16, suf), 1)
        row_seq = lax.rem(r_id // heads_dev, quad)
        for k in range(nquads):
            q = jnp.concatenate([qlat[l, g, k * 16 : (k + 1) * 16, :] for g in range(groups)], axis=0)
            qro = jnp.concatenate(
                [qrot[l, g * rows_g + k * 16 : g * rows_g + (k + 1) * 16, :] for g in range(groups)], axis=0
            )[:, :ROPE]
            keys = sl_v[l, k * quad : (k + 1) * quad].reshape(quad * suf, rank)
            turn = jnp.concatenate([sr_v[l, k * quad + u] for u in range(quad)], axis=1)
            s = (dot_nt(q, keys) + dot(qro, turn)) * SCALE
            live = jnp.concatenate(
                [(row_seq == u) & (lane < lengths[k * quad + u]) for u in range(quad)], axis=1
            )
            s = jnp.where(live, s, -jnp.inf)
            top = jnp.max(s, axis=1, keepdims=True)
            w = jnp.exp(s - top)
            tot = jnp.sum(w, axis=1, keepdims=True)
            o = dot(w.astype(BF16), keys)
            for g in range(groups):
                at = slice(g * rows_g + k * 16, g * rows_g + (k + 1) * 16)
                m_ref[l, at, :] = top[g * 16 : (g + 1) * 16]
                l_ref[l, at, :] = tot[g * 16 : (g + 1) * 16]
                acc[l, at, :] = o[g * 16 : (g + 1) * 16]

    def prefix(l):
        def some(b):
            for j in range(chunk):
                slot = table[l, b * chunk + j]
                kbuf[j * blk : (j + 1) * blk, :] = plat[l][slot]
                rbuf[:, j * blk : (j + 1) * blk] = prope[l][slot]
            q = qlat[l].reshape(rows, rank)
            s_ref[...] = (dot_nt(q, kbuf[...]) + dot(qrot[l][:, :ROPE], rbuf[...])) * SCALE
            old = m_ref[l]
            top = jnp.maximum(old, jnp.max(s_ref[...], axis=1, keepdims=True))
            w = jnp.exp(s_ref[...] - top)
            fac = jnp.exp(old - top)
            l_ref[l] = l_ref[l] * fac + jnp.sum(w, axis=1, keepdims=True)
            m_ref[l] = top
            acc[l] = acc[l] * fac + dot(w.astype(BF16), kbuf[...])

        if nblk == chunk:
            some(0)
        else:
            loop(0, nblk // chunk, some)
        res = acc[l] / l_ref[l]
        for c in range(rank // 128):
            scr[c] = res[:, c * 128 : (c + 1) * 128]
        for g in range(groups):
            for h in range(heads_dev):
                for c in range(rank // 128):
                    los[l, g, h * seqs : (h + 1) * seqs, c * 128 : (c + 1) * 128] = scr[
                        c, pl.ds(g * rows_g + h, seqs, stride=heads_dev), :
                    ].astype(BF16)
        for i in range(1, groups):
            send_lo(l, i).start()
        lr[l, dp] = los[l, dp]

    def own_out(l):
        return pltpu.make_async_copy(hvs.at[l, dp], out.at[l, :, cols(dp)], own_sem.at[1, l])

    def expand(l):
        c_vu[l].wait()
        for i in range(1, groups):
            recv_lo(l, i).wait_recv()
        for h in range(heads_dev):
            x = jnp.concatenate([lr[l, g, h * seqs : (h + 1) * seqs, :] for g in range(groups)], axis=0)
            v = dot(x, vu_v[l, h]).astype(BF16)
            for g in range(groups):
                hvs[l, g, :, h * VDIM : (h + 1) * VDIM] = v[g * seqs : (g + 1) * seqs]
        for i in range(1, groups):
            send_hv(l, i).start()
        own_out(l).start()

    mid = outer // 2 + 1
    for l in range(layers):
        absorb(l)
    for l in range(layers):
        forward_z(l, 1, 2)
        forward_y(l, 0, 1)
    for l in range(layers):
        forward_z(l, 2, mid)
        forward_y(l, 1, 2)
        if l == 0:
            suffix(l)
    for l in range(layers):
        forward_z(l, mid, outer)
        forward_y(l, 2, mid)
        forward_y(l, mid, outer)
        if l > 0:
            suffix(l)
        else:
            for cp in c_po:
                cp.wait()
        gather_c(l)
        prefix(l)
    for l in range(layers):
        expand(l)

    for l in range(layers):
        own_out(l).wait()
        for i in range(1, groups):
            recv_hv(l, i).wait_recv()
    for l in range(layers):
        for i in range(1, groups):
            send_q(l, i).wait_send()
            send_ql(l, i).wait_send()
            send_lo(l, i).wait_send()
            send_hv(l, i).wait_send()

        def last_z(i):
            for side in range(2):
                a, there = at_step(i, side)
                to = 1 - side

                @pl.when(there & has[to])
                def _():
                    for kind in range(2):
                        send_z(l, kind, to, a, own_piece(l, kind)).wait_send()

        def last_y(a):
            for kind in range(2):
                send_y(l, kind, a, own_piece(l, kind)).wait_send()

        for side in range(2):

            @pl.when(has[side])
            def _():
                for kind in range(2):
                    send_z(l, kind, side, za, own_piece(l, kind)).wait_send()

        def last_c(slot):
            for kind in range(2):
                send_c(l, kind, slot).wait_send()

        loop(1, outer, last_z)
        loop(0, outer, last_y)
        others(last_c)


def on_device(mesh, *args):
    qn, qr, ku, vu, pool_lat, pool_rope, table, suf_lat, suf_rope, lengths = args
    layers, seqs, _ = qn.shape
    groups = mesh.shape["dp"]
    ring = mesh.shape["head"]
    heads_dev, rank = ku.shape[1], ku.shape[3]
    per, blk = pool_lat.shape[1], pool_lat.shape[2]
    suf = suf_lat.shape[2]
    nblk = table.shape[1]
    chunk = max(c for c in range(1, 7) if nblk % c == 0)
    rows_g = seqs * heads_dev
    rows = groups * rows_g
    slots = per * ring
    outer = ring // 2
    dims = (layers, seqs, groups, heads_dev, rank, blk, suf, per, ring, nblk, chunk)
    V = pltpu.VMEM
    D = pltpu.SemaphoreType.DMA
    scratch = [
        V(qr.shape, BF16), V(ku.shape, BF16), V(vu.shape, BF16), V(suf_lat.shape, BF16), V(suf_rope.shape, BF16),
        *[V((slots, blk, rank), BF16) for _ in range(layers)],
        *[V((slots, ROPE, blk), BF16) for _ in range(layers)],
        V((layers, groups, seqs, heads_dev * NOPE), BF16),
        V((rank // 128, rows, 128), F32),
        V((layers, groups, rows_g, rank), BF16),
        V((layers, groups, rows_g, rank), BF16),
        V((rows, 128), F32),
        V((layers, rows, 128), BF16),
        V((layers, rows, 1), F32),
        V((layers, rows, 1), F32),
        V((layers, rows, rank), F32),
        V((rows, chunk * blk), F32),
        V((chunk * blk, rank), BF16),
        V((ROPE, chunk * blk), BF16),
        V((layers, groups, rows_g, rank), BF16),
        V((layers, groups, rows_g, rank), BF16),
        V((layers, groups, seqs, heads_dev * VDIM), BF16),
        D((5, layers)), D((2, layers)), D((2, layers)),
        *[D((layers, groups)) for _ in range(8)],
        D((layers, 2, 2, outer)),
        *[D((layers, 2, outer)) for _ in range(3)],
        *[D((layers, 2, ring)) for _ in range(2)],
    ]
    hbm = pl.BlockSpec(memory_space=pl.ANY)
    smem = pl.BlockSpec(memory_space=pltpu.SMEM)
    return pl.pallas_call(
        functools.partial(kernel, dims),
        out_shape=jax.ShapeDtypeStruct((layers, seqs, HEADS * VDIM), BF16),
        in_specs=[hbm] * 6 + [smem] + [hbm] * 2 + [smem],
        out_specs=hbm,
        scratch_shapes=scratch,
        compiler_params=pltpu.CompilerParams(
            collective_id=0, has_side_effects=True, vmem_limit_bytes=60 * 1024 * 1024
        ),
        name="latent_attention",
    )(*args)


def solution(mesh):
    return jax.shard_map(
        functools.partial(on_device, mesh),
        mesh=mesh,
        in_specs=(
            P(None, ("dp", "head"), None),
            P(None, ("dp", "head"), None),
            P(None, "dp", None, None),
            P(None, "dp", None, None),
            P(None, "head", None, None),
            P(None, "head", None, None),
            P(),
            P(None, ("dp", "head"), None, None),
            P(None, ("dp", "head"), None, None),
            P(("dp", "head")),
        ),
        out_specs=P(None, ("dp", "head"), None),
        check_vma=False,
    )
```

```python
import functools

import jax
import jax.numpy as jnp
from jax import lax
from jax.experimental import pallas as pl
from jax.experimental.pallas import tpu as pltpu
from jax.sharding import PartitionSpec as P

HEADS = 16
NOPE = 128
ROPE = 64
VDIM = 128
SCALE = (NOPE + ROPE) ** (-0.5)
MESH = pl.DeviceIdType.MESH
F32 = jnp.float32
BF16 = jnp.bfloat16
NT = (((1,), (1,)), ((), ()))


def dot(a, b):
    return jnp.dot(a, b, preferred_element_type=F32)


def dot_nt(a, b):
    return lax.dot_general(a, b, NT, preferred_element_type=F32)


def kernel(dims, *refs):
    (layers, seqs, groups, heads_dev, rank, blk, suf, per, ring, nblk, chunk) = dims
    it = iter(refs)

    def take(count):
        return [next(it) for _ in range(count)]

    qn, qr, ku, vu, pool_lat, pool_rope, table, suf_lat, suf_rope, lengths = take(10)
    (out,) = take(1)
    qr_v, ku_v, vu_v, sl_v, sr_v = take(5)
    plat = take(layers)
    prope = take(layers)
    hq, hr, scr, qls, qlat, qrf, qrot, hrot, m_ref, l_ref, acc, s_ref, kbuf, rbuf = take(14)
    los, lr, sts, strs, hvs = take(5)
    (
        loc_sem, pown_sem, own_sem,
        q_ss, q_rs, r_ss, r_rs, st_ss, st_rs, ql_ss, ql_rs, lo_ss, lo_rs, hv_ss, hv_rs,
        z_ss, z_rs, y_ss, y_rs, c_ss, c_rs,
    ) = take(21)

    dp = lax.axis_index("dp")
    hd = lax.axis_index("head")
    core = lax.rem(dp, 2)
    partner = dp + 1 - 2 * core
    za, yb = hd // 2, lax.rem(hd, 2)
    outer = ring // 2
    wide, wide_r = heads_dev * NOPE, heads_dev * ROPE
    rows_g = seqs * heads_dev
    rows = groups * rows_g
    quad = 16 // heads_dev
    nquads = seqs // quad

    local = []

    def fetch(src, dst, sem):
        cp = pltpu.make_async_copy(src, dst, sem)
        cp.start()
        return cp

    def own_q(l):
        return pltpu.make_async_copy(
            qn.at[l, :, pl.ds(pl.multiple_of(dp * wide, 128), wide)], hq.at[l, dp], own_sem.at[0, l]
        )

    def own_r(l):
        return pltpu.make_async_copy(
            qr.at[l, :, pl.ds(pl.multiple_of(dp * wide_r, 128), wide_r)], hr.at[l, dp], own_sem.at[2, l]
        )

    for l in range(layers):
        own_q(l).start()
        own_r(l).start()
    c_ku = [fetch(ku.at[l], ku_v.at[l], loc_sem.at[0, l]) for l in range(layers)]
    c_qr = fetch(qr, qr_v, loc_sem.at[1, 0])
    c_sl = [fetch(suf_lat.at[l], sl_v.at[l], loc_sem.at[2, l]) for l in range(layers)]
    c_sr = [fetch(suf_rope.at[l], sr_v.at[l], loc_sem.at[3, l]) for l in range(layers)]
    c_po = []
    for l in range(layers):
        mine = pl.ds(hd * per, per)
        c_po.append(fetch(pool_lat.at[l], plat[l].at[mine], pown_sem.at[0, l]))
        c_po.append(fetch(pool_rope.at[l], prope[l].at[mine], pown_sem.at[1, l]))
    c_vu = [fetch(vu.at[l], vu_v.at[l], loc_sem.at[4, l]) for l in range(layers)]

    barrier = pltpu.get_barrier_semaphore()

    def greet(d, h):
        pl.semaphore_signal(barrier, inc=1, device_id=(d, h), device_id_type=MESH)

    for i in range(1, groups):
        greet(lax.rem(dp + i, groups), hd)
    has = (za > 0, za < outer - 1)
    for side in range(2):
        pl.when(has[side])(lambda: greet(dp, (za + 2 * side - 1) * 2 + yb))
    greet(dp, za * 2 + 1 - yb)
    sides = (za + outer - 1) // outer + (2 * outer - 2 - za) // outer
    pl.semaphore_wait(barrier, groups + sides)

    def remote(src, dst, ss, rs, d, h):
        return pltpu.make_async_remote_copy(
            src_ref=src, dst_ref=dst, send_sem=ss, recv_sem=rs, device_id=(d, h), device_id_type=MESH
        )

    def peer(i):
        return lax.rem(dp + i, groups)

    def send_q(l, i):
        j = peer(i)
        return remote(
            qn.at[l, :, pl.ds(pl.multiple_of(j * wide, 128), wide)], hq.at[l, dp],
            q_ss.at[l, j], q_rs.at[l, dp], j, hd,
        )

    def recv_q(l, i):
        j = peer(i)
        return remote(hq.at[l, j], hq.at[l, j], q_ss.at[l, j], q_rs.at[l, j], j, hd)

    def send_r(l, i):
        j = peer(i)
        return remote(
            qr.at[l, :, pl.ds(pl.multiple_of(j * wide_r, 128), wide_r)], hr.at[l, dp],
            r_ss.at[l, j], r_rs.at[l, dp], j, hd,
        )

    def recv_r(l, i):
        j = peer(i)
        return remote(hr.at[l, j], hr.at[l, j], r_ss.at[l, j], r_rs.at[l, j], j, hd)

    def pair(sends, buf, ss, rs):
        def send(l, i):
            j = peer(i)
            return remote(sends.at[l, j], buf.at[l, dp], ss.at[l, j], rs.at[l, dp], j, hd)

        def recv(l, i):
            j = peer(i)
            return remote(sends.at[l, j], buf.at[l, j], ss.at[l, j], rs.at[l, j], j, hd)

        return send, recv

    send_ql, recv_ql = pair(qls, qlat, ql_ss, ql_rs)
    send_lo, recv_lo = pair(los, lr, lo_ss, lo_rs)
    send_st, recv_st = pair(sts, strs, st_ss, st_rs)

    def cols(j):
        return pl.ds(pl.multiple_of(j * heads_dev * VDIM, 128), heads_dev * VDIM)

    def send_hv(l, i):
        j = peer(i)
        return remote(hvs.at[l, j], out.at[l, :, cols(dp)], hv_ss.at[l, j], hv_rs.at[l, dp], j, hd)

    def recv_hv(l, i):
        j = peer(i)
        return remote(hvs.at[l, j], out.at[l, :, cols(j)], hv_ss.at[l, j], hv_rs.at[l, j], j, hd)

    def half(kind, c):
        size = (blk if kind == 0 else ROPE) // 2
        return pl.ds(pl.multiple_of(c * size, 16), size)

    def pool_at(l, kind, slot, c):
        buf = (plat if kind == 0 else prope)[l]
        return buf.at[pl.ds(slot * per, per), half(kind, c)]

    def own_piece(l, kind):
        return (pool_lat if kind == 0 else pool_rope).at[l, :, half(kind, core)]

    def send_z(l, kind, side, a, src):
        return remote(
            src, pool_at(l, kind, a * 2 + yb, core),
            z_ss.at[l, kind, side, a], z_rs.at[l, kind, a], dp, (za + 2 * side - 1) * 2 + yb,
        )

    def recv_z(l, kind, side, a):
        return remote(
            own_piece(l, kind), pool_at(l, kind, a * 2 + yb, core),
            z_ss.at[l, kind, side, a], z_rs.at[l, kind, a], dp, (za + 2 * side - 1) * 2 + yb,
        )

    def send_y(l, kind, a, src):
        return remote(
            src, pool_at(l, kind, a * 2 + yb, core),
            y_ss.at[l, kind, a], y_rs.at[l, kind, a], dp, za * 2 + 1 - yb,
        )

    def recv_y(l, kind, a):
        return remote(
            own_piece(l, kind), pool_at(l, kind, a * 2 + 1 - yb, core),
            y_ss.at[l, kind, a], y_rs.at[l, kind, a], dp, za * 2 + 1 - yb,
        )

    def send_c(l, kind, slot):
        piece = pool_at(l, kind, slot, core)
        return remote(piece, piece, c_ss.at[l, kind, slot], c_rs.at[l, kind, slot], partner, hd)

    def recv_c(l, kind, slot):
        piece = pool_at(l, kind, slot, 1 - core)
        return remote(piece, piece, c_ss.at[l, kind, slot], c_rs.at[l, kind, slot], partner, hd)

    def loop(low, high, body):
        def step(i, carry):
            body(i)
            return carry

        lax.fori_loop(low, high, step, 0)

    for l in range(layers):
        for i in range(1, groups):
            send_q(l, i).start()
            send_r(l, i).start()
    for l in range(layers):
        for kind in range(2):
            send_y(l, kind, za, own_piece(l, kind)).start()
            for side in range(2):
                pl.when(has[side])(lambda: send_z(l, kind, side, za, own_piece(l, kind)).start())

    def at_step(i, side):
        a = za + (2 * side - 1) * i
        return a, (a >= 0 if side == 0 else a < outer)

    def span(low, high, body):
        if high - low == 1:
            body(low)
        else:
            loop(low, high, body)

    def forward_z(l, low, high):
        def body(i):
            for side in range(2):
                a, there = at_step(i, side)

                @pl.when(there)
                def _():
                    for kind in range(2):
                        recv_z(l, kind, side, a).wait_recv()
                        piece = pool_at(l, kind, a * 2 + yb, core)
                        pl.when(has[1 - side])(lambda: send_z(l, kind, 1 - side, a, piece).start())
                        send_y(l, kind, a, piece).start()
                        send_c(l, kind, a * 2 + yb).start()

        span(low, high, body)

    def pass_y(l, a):
        for kind in range(2):
            recv_y(l, kind, a).wait_recv()
            send_c(l, kind, a * 2 + 1 - yb).start()

    def forward_y(l, low, high):
        def body(i):
            for side in range(2):
                a, there = at_step(i, side)
                pl.when(there)(lambda: pass_y(l, a))

        if low == 0:
            pass_y(l, za)
        else:
            span(low, high, body)

    def others(body):
        loop(1, ring, lambda i: body(lax.rem(hd + i, ring)))

    def gather_c(l):
        def body(slot):
            for kind in range(2):
                recv_c(l, kind, slot).wait_recv()

        others(body)

    def rotary(part, to):
        for g in range(groups):
            for h in range(heads_dev):
                at = h * ROPE
                piece = part(g, at // 128 * 128).astype(F32)
                if at % 128:
                    piece = pltpu.roll(piece, 128 - at % 128, 1)
                qrf[pl.ds(g * rows_g + h, seqs, stride=heads_dev), :] = piece
        to[...] = qrf[...].astype(BF16)

    c_qr.wait()
    for l in range(layers):
        rotary(lambda g, at: qr_v[l, :, g * wide_r + at : g * wide_r + at + 128], qrot.at[l])

    def held_rotary(l):
        own_r(l).wait()
        for i in range(1, groups):
            recv_r(l, i).wait_recv()
        rotary(lambda g, at: hr[l, g, :, at : at + 128], hrot.at[l])

    def absorb(l):
        own_q(l).wait()
        for i in range(1, groups):
            recv_q(l, i).wait_recv()
        c_ku[l].wait()
        for h in range(heads_dev):
            x = jnp.concatenate([hq[l, g, :, h * NOPE : (h + 1) * NOPE] for g in range(groups)], axis=0)
            r = dot(x, ku_v[l, h])
            for c in range(rank // 128):
                scr[c, pl.ds(h, groups * seqs, stride=heads_dev), :] = r[:, c * 128 : (c + 1) * 128]
        for g in range(groups):
            for c in range(rank // 128):
                qls[l, g, :, c * 128 : (c + 1) * 128] = scr[c, g * rows_g : (g + 1) * rows_g, :].astype(BF16)
        for i in range(1, groups):
            send_ql(l, i).start()
        qlat[l, dp] = qls[l, dp]

    def suffix(l):
        c_sl[l].wait()
        c_sr[l].wait()
        for i in range(1, groups):
            recv_ql(l, i).wait_recv()
        r_id = lax.broadcasted_iota(jnp.int32, (groups * 16, suf), 0)
        lane = lax.broadcasted_iota(jnp.int32, (groups * 16, suf), 1)
        row_seq = lax.rem(r_id // heads_dev, quad)
        for k in range(nquads):
            q = jnp.concatenate([qlat[l, g, k * 16 : (k + 1) * 16, :] for g in range(groups)], axis=0)
            qro = jnp.concatenate(
                [qrot[l, g * rows_g + k * 16 : g * rows_g + (k + 1) * 16, :] for g in range(groups)], axis=0
            )[:, :ROPE]
            keys = sl_v[l, k * quad : (k + 1) * quad].reshape(quad * suf, rank)
            turn = jnp.concatenate([sr_v[l, k * quad + u] for u in range(quad)], axis=1)
            s = (dot_nt(q, keys) + dot(qro, turn)) * SCALE
            live = jnp.concatenate(
                [(row_seq == u) & (lane < lengths[k * quad + u]) for u in range(quad)], axis=1
            )
            s = jnp.where(live, s, -jnp.inf)
            top = jnp.max(s, axis=1, keepdims=True)
            w = jnp.exp(s - top)
            tot = jnp.sum(w, axis=1, keepdims=True)
            o = dot(w.astype(BF16), keys)
            o = o / tot
            lse = top + jnp.log(tot)
            for g in range(groups):
                at = slice(k * 16, (k + 1) * 16)
                los[l, g, at, :] = o[g * 16 : (g + 1) * 16].astype(BF16)
                m_ref[l, g * rows_g + k * 16 : g * rows_g + (k + 1) * 16, :] = lse[g * 16 : (g + 1) * 16]
        for g in range(groups):
            column = jnp.broadcast_to(m_ref[l, g * rows_g : (g + 1) * rows_g, :], (rows_g, 128))
            sts[l, g] = jnp.concatenate([column] * (128 // rows_g), axis=0).T[:8]
        for i in range(1, groups):
            send_lo(l, i).start()
            send_st(l, i).start()
        lr[l, dp] = los[l, dp]
        strs[l, dp] = sts[l, dp]

    def prefix(l):
        def some(b, start):
            for j in range(chunk):
                slot = table[l, b * chunk + j]
                kbuf[j * blk : (j + 1) * blk, :] = plat[l][slot]
                rbuf[:, j * blk : (j + 1) * blk] = prope[l][slot]
            q = qls[l].reshape(rows, rank)
            s_ref[...] = (dot_nt(q, kbuf[...]) + dot(hrot[l][:, :ROPE], rbuf[...])) * SCALE
            top = jnp.max(s_ref[...], axis=1, keepdims=True)
            if not start:
                top = jnp.maximum(m_ref[l], top)
            w = jnp.exp(s_ref[...] - top)
            tot = jnp.sum(w, axis=1, keepdims=True)
            o = dot(w.astype(BF16), kbuf[...])
            if not start:
                fac = jnp.exp(m_ref[l] - top)
                tot = l_ref[l] * fac + tot
                o = acc[l] * fac + o
            l_ref[l] = tot
            m_ref[l] = top
            acc[l] = o

        some(0, True)
        if nblk > chunk:
            loop(1, nblk // chunk, lambda b: some(b, False))

    def own_out(l):
        return pltpu.make_async_copy(hvs.at[l, dp], out.at[l, :, cols(dp)], own_sem.at[1, l])

    def expand(l):
        c_vu[l].wait()
        for i in range(1, groups):
            recv_lo(l, i).wait_recv()
            recv_st(l, i).wait_recv()
        for g in range(groups):
            at = slice(g * rows_g, (g + 1) * rows_g)
            lse = jnp.broadcast_to(strs[l, g, 0:1, :], (128, 128)).T[:rows_g, 0:1]
            old = m_ref[l, at, :]
            top = jnp.maximum(old, lse)
            own, pre = jnp.exp(lse - top), jnp.exp(old - top)
            inv = 1.0 / (own + l_ref[l, at, :] * pre)
            res = lr[l, g].astype(F32) * (own * inv) + acc[l, at, :] * (pre * inv)
            for c in range(rank // 128):
                scr[c, at, :] = res[:, c * 128 : (c + 1) * 128]
        for h in range(heads_dev):
            x = jnp.concatenate(
                [scr[c, pl.ds(h, groups * seqs, stride=heads_dev), :] for c in range(rank // 128)], axis=1
            ).astype(BF16)
            v = dot(x, vu_v[l, h]).astype(BF16)
            for g in range(groups):
                hvs[l, g, :, h * VDIM : (h + 1) * VDIM] = v[g * seqs : (g + 1) * seqs]
        for i in range(1, groups):
            send_hv(l, i).start()
        own_out(l).start()

    mid = outer // 2 + 1
    for l in range(layers):
        absorb(l)
    for l in range(layers):
        forward_z(l, 1, 2)
        forward_y(l, 0, 1)
        held_rotary(l)
    for l in range(layers):
        forward_z(l, 2, mid)
        forward_y(l, 1, 2)
        if l == 0:
            suffix(l)
    for l in range(layers):
        forward_z(l, mid, outer)
        forward_y(l, 2, mid)
        if l > 0:
            suffix(l)
    for cp in c_po:
        cp.wait()
    for l in range(layers):
        forward_y(l, mid, outer)
    for l in range(layers):
        gather_c(l)
        prefix(l)
        expand(l)

    for l in range(layers):
        own_out(l).wait()
        for i in range(1, groups):
            recv_hv(l, i).wait_recv()
    for l in range(layers):
        for i in range(1, groups):
            send_q(l, i).wait_send()
            send_r(l, i).wait_send()
            send_st(l, i).wait_send()
            send_ql(l, i).wait_send()
            send_lo(l, i).wait_send()
            send_hv(l, i).wait_send()

        def last_z(i):
            for side in range(2):
                a, there = at_step(i, side)
                to = 1 - side

                @pl.when(there & has[to])
                def _():
                    for kind in range(2):
                        send_z(l, kind, to, a, own_piece(l, kind)).wait_send()

        def last_y(a):
            for kind in range(2):
                send_y(l, kind, a, own_piece(l, kind)).wait_send()

        for side in range(2):

            @pl.when(has[side])
            def _():
                for kind in range(2):
                    send_z(l, kind, side, za, own_piece(l, kind)).wait_send()

        def last_c(slot):
            for kind in range(2):
                send_c(l, kind, slot).wait_send()

        loop(1, outer, last_z)
        loop(0, outer, last_y)
        others(last_c)


def on_device(mesh, *args):
    qn, qr, ku, vu, pool_lat, pool_rope, table, suf_lat, suf_rope, lengths = args
    layers, seqs, _ = qn.shape
    groups = mesh.shape["dp"]
    ring = mesh.shape["head"]
    heads_dev, rank = ku.shape[1], ku.shape[3]
    per, blk = pool_lat.shape[1], pool_lat.shape[2]
    suf = suf_lat.shape[2]
    nblk = table.shape[1]
    chunk = max(c for c in range(1, 7) if nblk % c == 0)
    rows_g = seqs * heads_dev
    rows = groups * rows_g
    slots = per * ring
    outer = ring // 2
    dims = (layers, seqs, groups, heads_dev, rank, blk, suf, per, ring, nblk, chunk)
    V = pltpu.VMEM
    D = pltpu.SemaphoreType.DMA
    scratch = [
        V(qr.shape, BF16), V(ku.shape, BF16), V(vu.shape, BF16), V(suf_lat.shape, BF16), V(suf_rope.shape, BF16),
        *[V((slots, blk, rank), BF16) for _ in range(layers)],
        *[V((slots, ROPE, blk), BF16) for _ in range(layers)],
        V((layers, groups, seqs, heads_dev * NOPE), BF16),
        V((layers, groups, seqs, heads_dev * ROPE), BF16),
        V((rank // 128, rows, 128), F32),
        V((layers, groups, rows_g, rank), BF16),
        V((layers, groups, rows_g, rank), BF16),
        V((rows, 128), F32),
        V((layers, rows, 128), BF16),
        V((layers, rows, 128), BF16),
        V((layers, rows, 1), F32),
        V((layers, rows, 1), F32),
        V((layers, rows, rank), F32),
        V((rows, chunk * blk), F32),
        V((chunk * blk, rank), BF16),
        V((ROPE, chunk * blk), BF16),
        V((layers, groups, rows_g, rank), BF16),
        V((layers, groups, rows_g, rank), BF16),
        V((layers, groups, 8, 128), F32),
        V((layers, groups, 8, 128), F32),
        V((layers, groups, seqs, heads_dev * VDIM), BF16),
        D((5, layers)), D((2, layers)), D((3, layers)),
        *[D((layers, groups)) for _ in range(12)],
        D((layers, 2, 2, outer)),
        *[D((layers, 2, outer)) for _ in range(3)],
        *[D((layers, 2, ring)) for _ in range(2)],
    ]
    hbm = pl.BlockSpec(memory_space=pl.ANY)
    smem = pl.BlockSpec(memory_space=pltpu.SMEM)
    return pl.pallas_call(
        functools.partial(kernel, dims),
        out_shape=jax.ShapeDtypeStruct((layers, seqs, HEADS * VDIM), BF16),
        in_specs=[hbm] * 6 + [smem] + [hbm] * 2 + [smem],
        out_specs=hbm,
        scratch_shapes=scratch,
        compiler_params=pltpu.CompilerParams(
            collective_id=0, has_side_effects=True, vmem_limit_bytes=60 * 1024 * 1024
        ),
        name="latent_attention",
    )(*args)


def solution(mesh):
    return jax.shard_map(
        functools.partial(on_device, mesh),
        mesh=mesh,
        in_specs=(
            P(None, ("dp", "head"), None),
            P(None, ("dp", "head"), None),
            P(None, "dp", None, None),
            P(None, "dp", None, None),
            P(None, "head", None, None),
            P(None, "head", None, None),
            P(),
            P(None, ("dp", "head"), None, None),
            P(None, ("dp", "head"), None, None),
            P(("dp", "head")),
        ),
        out_specs=P(None, ("dp", "head"), None),
        check_vma=False,
    )
```

```python
import functools

import jax
import jax.numpy as jnp
from jax import lax
from jax.experimental import pallas as pl
from jax.experimental.pallas import tpu as pltpu
from jax.sharding import PartitionSpec as P

HEADS = 16
NOPE = 128
ROPE = 64
VDIM = 128
SCALE = (NOPE + ROPE) ** (-0.5)
MESH = pl.DeviceIdType.MESH
KINDS = 3
F32 = jnp.float32
BF16 = jnp.bfloat16
NT = (((1,), (1,)), ((), ()))


def dot(a, b):
    return jnp.dot(a, b, preferred_element_type=F32)


def dot_nt(a, b):
    return lax.dot_general(a, b, NT, preferred_element_type=F32)


def kernel(dims, *refs):
    (layers, seqs, groups, heads_dev, rank, blk, suf, per, ring, nblk, chunk) = dims
    it = iter(refs)

    def take(count):
        return [next(it) for _ in range(count)]

    qn, qr, ku, vu, pool_lat, pool_rope, table, suf_lat, suf_rope, lengths = take(10)
    (out,) = take(1)
    qr_v, ku_v, vu_v, sl_v, sr_v = take(5)
    plat = take(layers)
    prope = take(layers)
    hq, hr, scr, qls, qlat, qrf, qrot, hrot, m_ref, l_ref, acc, s_ref, kbuf, rbuf = take(14)
    los, lr, sts, strs, hvs = take(5)
    (
        loc_sem, pown_sem, own_sem,
        q_ss, q_rs, r_ss, r_rs, st_ss, st_rs, ql_ss, ql_rs, lo_ss, lo_rs, hv_ss, hv_rs,
        z_ss, z_rs, y_ss, y_rs, c_ss, c_rs,
    ) = take(21)

    dp = lax.axis_index("dp")
    hd = lax.axis_index("head")
    core = lax.rem(dp, 2)
    partner = dp + 1 - 2 * core
    za, yb = hd // 2, lax.rem(hd, 2)
    outer = ring // 2
    wide, wide_r = heads_dev * NOPE, heads_dev * ROPE
    rows_g = seqs * heads_dev
    rows = groups * rows_g
    quad = 16 // heads_dev
    nquads = seqs // quad

    local = []

    def fetch(src, dst, sem):
        cp = pltpu.make_async_copy(src, dst, sem)
        cp.start()
        return cp

    def own_q(l):
        return pltpu.make_async_copy(
            qn.at[l, :, pl.ds(pl.multiple_of(dp * wide, 128), wide)], hq.at[l, dp], own_sem.at[0, l]
        )

    def own_r(l):
        return pltpu.make_async_copy(
            qr.at[l, :, pl.ds(pl.multiple_of(dp * wide_r, 128), wide_r)], hr.at[l, dp], own_sem.at[2, l]
        )

    for l in range(layers):
        own_q(l).start()
        own_r(l).start()
    c_ku = [fetch(ku.at[l], ku_v.at[l], loc_sem.at[0, l]) for l in range(layers)]
    c_qr = fetch(qr, qr_v, loc_sem.at[1, 0])

    barrier = pltpu.get_barrier_semaphore()

    def greet(d, h):
        pl.semaphore_signal(barrier, inc=1, device_id=(d, h), device_id_type=MESH)

    for i in range(1, groups):
        greet(lax.rem(dp + i, groups), hd)
    has = (za > 0, za < outer - 1)
    for side in range(2):
        pl.when(has[side])(lambda: greet(dp, (za + 2 * side - 1) * 2 + yb))
    greet(dp, za * 2 + 1 - yb)
    sides = (za + outer - 1) // outer + (2 * outer - 2 - za) // outer
    pl.semaphore_wait(barrier, groups + sides)

    def remote(src, dst, ss, rs, d, h):
        return pltpu.make_async_remote_copy(
            src_ref=src, dst_ref=dst, send_sem=ss, recv_sem=rs, device_id=(d, h), device_id_type=MESH
        )

    def peer(i):
        return lax.rem(dp + i, groups)

    def send_q(l, i):
        j = peer(i)
        return remote(
            qn.at[l, :, pl.ds(pl.multiple_of(j * wide, 128), wide)], hq.at[l, dp],
            q_ss.at[l, j], q_rs.at[l, dp], j, hd,
        )

    def recv_q(l, i):
        j = peer(i)
        return remote(hq.at[l, j], hq.at[l, j], q_ss.at[l, j], q_rs.at[l, j], j, hd)

    def send_r(l, i):
        j = peer(i)
        return remote(
            qr.at[l, :, pl.ds(pl.multiple_of(j * wide_r, 128), wide_r)], hr.at[l, dp],
            r_ss.at[l, j], r_rs.at[l, dp], j, hd,
        )

    def recv_r(l, i):
        j = peer(i)
        return remote(hr.at[l, j], hr.at[l, j], r_ss.at[l, j], r_rs.at[l, j], j, hd)

    def pair(sends, buf, ss, rs):
        def send(l, i):
            j = peer(i)
            return remote(sends.at[l, j], buf.at[l, dp], ss.at[l, j], rs.at[l, dp], j, hd)

        def recv(l, i):
            j = peer(i)
            return remote(sends.at[l, j], buf.at[l, j], ss.at[l, j], rs.at[l, j], j, hd)

        return send, recv

    send_ql, recv_ql = pair(qls, qlat, ql_ss, ql_rs)
    send_lo, recv_lo = pair(los, lr, lo_ss, lo_rs)
    send_st, recv_st = pair(sts, strs, st_ss, st_rs)

    def cols(j):
        return pl.ds(pl.multiple_of(j * heads_dev * VDIM, 128), heads_dev * VDIM)

    def send_hv(l, i):
        j = peer(i)
        return remote(hvs.at[l, j], out.at[l, :, cols(dp)], hv_ss.at[l, j], hv_rs.at[l, dp], j, hd)

    def recv_hv(l, i):
        j = peer(i)
        return remote(hvs.at[l, j], out.at[l, :, cols(j)], hv_ss.at[l, j], hv_rs.at[l, j], j, hd)

    def half(kind, c):
        parts = KINDS - 1 if kind < KINDS - 1 else 1
        size = (blk if kind < KINDS - 1 else ROPE) // 2 // parts
        at = (c * parts + (kind if kind < KINDS - 1 else 0)) * size
        return pl.ds(pl.multiple_of(at, 16), size)

    def pool_at(l, kind, slot, c):
        buf = (plat if kind < KINDS - 1 else prope)[l]
        return buf.at[pl.ds(slot * per, per), half(kind, c)]

    def own_piece(l, kind):
        return (pool_lat if kind < KINDS - 1 else pool_rope).at[l, :, half(kind, core)]

    def send_z(l, kind, side, a, src):
        return remote(
            src, pool_at(l, kind, a * 2 + yb, core),
            z_ss.at[l, kind, side, a], z_rs.at[l, kind, a], dp, (za + 2 * side - 1) * 2 + yb,
        )

    def recv_z(l, kind, side, a):
        return remote(
            own_piece(l, kind), pool_at(l, kind, a * 2 + yb, core),
            z_ss.at[l, kind, side, a], z_rs.at[l, kind, a], dp, (za + 2 * side - 1) * 2 + yb,
        )

    def send_y(l, kind, a, src):
        return remote(
            src, pool_at(l, kind, a * 2 + yb, core),
            y_ss.at[l, kind, a], y_rs.at[l, kind, a], dp, za * 2 + 1 - yb,
        )

    def recv_y(l, kind, a):
        return remote(
            own_piece(l, kind), pool_at(l, kind, a * 2 + 1 - yb, core),
            y_ss.at[l, kind, a], y_rs.at[l, kind, a], dp, za * 2 + 1 - yb,
        )

    def send_c(l, kind, slot):
        piece = pool_at(l, kind, slot, core)
        return remote(piece, piece, c_ss.at[l, kind, slot], c_rs.at[l, kind, slot], partner, hd)

    def recv_c(l, kind, slot):
        piece = pool_at(l, kind, slot, 1 - core)
        return remote(piece, piece, c_ss.at[l, kind, slot], c_rs.at[l, kind, slot], partner, hd)

    def loop(low, high, body):
        def step(i, carry):
            body(i)
            return carry

        lax.fori_loop(low, high, step, 0)

    for l in range(layers):
        for i in range(1, groups):
            send_q(l, i).start()
            send_r(l, i).start()
    for l in range(layers):
        for kind in range(KINDS):
            send_y(l, kind, za, own_piece(l, kind)).start()
            for side in range(2):
                pl.when(has[side])(lambda: send_z(l, kind, side, za, own_piece(l, kind)).start())

    c_sl = [fetch(suf_lat.at[l], sl_v.at[l], loc_sem.at[2, l]) for l in range(layers)]
    c_sr = [fetch(suf_rope.at[l], sr_v.at[l], loc_sem.at[3, l]) for l in range(layers)]
    c_po = []
    for l in range(layers):
        mine = pl.ds(hd * per, per)
        c_po.append(fetch(pool_lat.at[l], plat[l].at[mine], pown_sem.at[0, l]))
        c_po.append(fetch(pool_rope.at[l], prope[l].at[mine], pown_sem.at[1, l]))
    c_vu = [fetch(vu.at[l], vu_v.at[l], loc_sem.at[4, l]) for l in range(layers)]

    def at_step(i, side):
        a = za + (2 * side - 1) * i
        return a, (a >= 0 if side == 0 else a < outer)

    def span(low, high, body):
        if high - low == 1:
            body(low)
        else:
            loop(low, high, body)

    def forward_z(l, low, high):
        def body(i):
            for side in range(2):
                a, there = at_step(i, side)

                @pl.when(there)
                def _():
                    for kind in range(KINDS):
                        recv_z(l, kind, side, a).wait_recv()
                        piece = pool_at(l, kind, a * 2 + yb, core)
                        pl.when(has[1 - side])(lambda: send_z(l, kind, 1 - side, a, piece).start())
                        send_y(l, kind, a, piece).start()
                        send_c(l, kind, a * 2 + yb).start()

        span(low, high, body)

    def pass_y(l, a):
        for kind in range(KINDS):
            recv_y(l, kind, a).wait_recv()
            send_c(l, kind, a * 2 + 1 - yb).start()

    def forward_y(l, low, high):
        def body(i):
            for side in range(2):
                a, there = at_step(i, side)
                pl.when(there)(lambda: pass_y(l, a))

        if low == 0:
            pass_y(l, za)
        else:
            span(low, high, body)

    def others(body):
        loop(1, ring, lambda i: body(lax.rem(hd + i, ring)))

    def gather_c(l):
        def body(slot):
            for kind in range(KINDS):
                recv_c(l, kind, slot).wait_recv()

        others(body)

    def rotary(part, to):
        for g in range(groups):
            for h in range(heads_dev):
                at = h * ROPE
                piece = part(g, at // 128 * 128).astype(F32)
                if at % 128:
                    piece = pltpu.roll(piece, 128 - at % 128, 1)
                qrf[pl.ds(g * rows_g + h, seqs, stride=heads_dev), :] = piece
        to[...] = qrf[...].astype(BF16)

    c_qr.wait()
    for l in range(layers):
        rotary(lambda g, at: qr_v[l, :, g * wide_r + at : g * wide_r + at + 128], qrot.at[l])

    def held_rotary(l):
        own_r(l).wait()
        for i in range(1, groups):
            recv_r(l, i).wait_recv()
        rotary(lambda g, at: hr[l, g, :, at : at + 128], hrot.at[l])

    def absorb(l):
        own_q(l).wait()
        for i in range(1, groups):
            recv_q(l, i).wait_recv()
        c_ku[l].wait()
        for h in range(heads_dev):
            x = jnp.concatenate([hq[l, g, :, h * NOPE : (h + 1) * NOPE] for g in range(groups)], axis=0)
            r = dot(x, ku_v[l, h])
            for c in range(rank // 128):
                scr[c, pl.ds(h, groups * seqs, stride=heads_dev), :] = r[:, c * 128 : (c + 1) * 128]
        for g in range(groups):
            for c in range(rank // 128):
                qls[l, g, :, c * 128 : (c + 1) * 128] = scr[c, g * rows_g : (g + 1) * rows_g, :].astype(BF16)
        for i in range(1, groups):
            send_ql(l, i).start()
        qlat[l, dp] = qls[l, dp]

    def suffix(l):
        c_sl[l].wait()
        c_sr[l].wait()
        for i in range(1, groups):
            recv_ql(l, i).wait_recv()
        r_id = lax.broadcasted_iota(jnp.int32, (groups * 16, suf), 0)
        lane = lax.broadcasted_iota(jnp.int32, (groups * 16, suf), 1)
        row_seq = lax.rem(r_id // heads_dev, quad)
        for k in range(nquads):
            q = jnp.concatenate([qlat[l, g, k * 16 : (k + 1) * 16, :] for g in range(groups)], axis=0)
            qro = jnp.concatenate(
                [qrot[l, g * rows_g + k * 16 : g * rows_g + (k + 1) * 16, :] for g in range(groups)], axis=0
            )[:, :ROPE]
            keys = sl_v[l, k * quad : (k + 1) * quad].reshape(quad * suf, rank)
            turn = jnp.concatenate([sr_v[l, k * quad + u] for u in range(quad)], axis=1)
            s = (dot_nt(q, keys) + dot(qro, turn)) * SCALE
            live = jnp.concatenate(
                [(row_seq == u) & (lane < lengths[k * quad + u]) for u in range(quad)], axis=1
            )
            s = jnp.where(live, s, -jnp.inf)
            top = jnp.max(s, axis=1, keepdims=True)
            w = jnp.exp(s - top)
            tot = jnp.sum(w, axis=1, keepdims=True)
            o = dot(w.astype(BF16), keys)
            o = o / tot
            lse = top + jnp.log(tot)
            for g in range(groups):
                at = slice(k * 16, (k + 1) * 16)
                los[l, g, at, :] = o[g * 16 : (g + 1) * 16].astype(BF16)
                m_ref[l, g * rows_g + k * 16 : g * rows_g + (k + 1) * 16, :] = lse[g * 16 : (g + 1) * 16]
        for g in range(groups):
            column = jnp.broadcast_to(m_ref[l, g * rows_g : (g + 1) * rows_g, :], (rows_g, 128))
            sts[l, g] = jnp.concatenate([column] * (128 // rows_g), axis=0).T[:8]
        for i in range(1, groups):
            send_lo(l, i).start()
            send_st(l, i).start()
        lr[l, dp] = los[l, dp]
        strs[l, dp] = sts[l, dp]

    def prefix(l):
        def some(b, start):
            for j in range(chunk):
                slot = table[l, b * chunk + j]
                kbuf[j * blk : (j + 1) * blk, :] = plat[l][slot]
                rbuf[:, j * blk : (j + 1) * blk] = prope[l][slot]
            q = qls[l].reshape(rows, rank)
            s_ref[...] = (dot_nt(q, kbuf[...]) + dot(hrot[l][:, :ROPE], rbuf[...])) * SCALE
            top = jnp.max(s_ref[...], axis=1, keepdims=True)
            if not start:
                top = jnp.maximum(m_ref[l], top)
            w = jnp.exp(s_ref[...] - top)
            tot = jnp.sum(w, axis=1, keepdims=True)
            o = dot(w.astype(BF16), kbuf[...])
            if not start:
                fac = jnp.exp(m_ref[l] - top)
                tot = l_ref[l] * fac + tot
                o = acc[l] * fac + o
            l_ref[l] = tot
            m_ref[l] = top
            acc[l] = o

        some(0, True)
        if nblk > chunk:
            loop(1, nblk // chunk, lambda b: some(b, False))

    def own_out(l):
        return pltpu.make_async_copy(hvs.at[l, dp], out.at[l, :, cols(dp)], own_sem.at[1, l])

    def expand(l):
        c_vu[l].wait()
        for i in range(1, groups):
            recv_lo(l, i).wait_recv()
            recv_st(l, i).wait_recv()
        for g in range(groups):
            at = slice(g * rows_g, (g + 1) * rows_g)
            lse = jnp.broadcast_to(strs[l, g, 0:1, :], (128, 128)).T[:rows_g, 0:1]
            old = m_ref[l, at, :]
            top = jnp.maximum(old, lse)
            own, pre = jnp.exp(lse - top), jnp.exp(old - top)
            inv = 1.0 / (own + l_ref[l, at, :] * pre)
            res = lr[l, g].astype(F32) * (own * inv) + acc[l, at, :] * (pre * inv)
            for c in range(rank // 128):
                scr[c, at, :] = res[:, c * 128 : (c + 1) * 128]
        for h in range(heads_dev):
            x = jnp.concatenate(
                [scr[c, pl.ds(h, groups * seqs, stride=heads_dev), :] for c in range(rank // 128)], axis=1
            ).astype(BF16)
            v = dot(x, vu_v[l, h]).astype(BF16)
            for g in range(groups):
                hvs[l, g, :, h * VDIM : (h + 1) * VDIM] = v[g * seqs : (g + 1) * seqs]
        for i in range(1, groups):
            send_hv(l, i).start()
        own_out(l).start()

    mid = outer // 2 + 1
    for l in range(layers):
        absorb(l)
    for l in range(layers):
        forward_z(l, 1, 2)
        forward_y(l, 0, 1)
        held_rotary(l)
    for l in range(layers):
        forward_z(l, 2, mid)
        forward_y(l, 1, 2)
        if l == 0:
            suffix(l)
    for l in range(layers):
        forward_z(l, mid, outer)
        forward_y(l, 2, mid)
        if l > 0:
            suffix(l)
    for cp in c_po:
        cp.wait()
    for l in range(layers):
        forward_y(l, mid, outer)
    for l in range(layers):
        gather_c(l)
        prefix(l)
        expand(l)

    for l in range(layers):
        own_out(l).wait()
        for i in range(1, groups):
            recv_hv(l, i).wait_recv()
    for l in range(layers):
        for i in range(1, groups):
            send_q(l, i).wait_send()
            send_r(l, i).wait_send()
            send_st(l, i).wait_send()
            send_ql(l, i).wait_send()
            send_lo(l, i).wait_send()
            send_hv(l, i).wait_send()

        def last_z(i):
            for side in range(2):
                a, there = at_step(i, side)
                to = 1 - side

                @pl.when(there & has[to])
                def _():
                    for kind in range(KINDS):
                        send_z(l, kind, to, a, own_piece(l, kind)).wait_send()

        def last_y(a):
            for kind in range(KINDS):
                send_y(l, kind, a, own_piece(l, kind)).wait_send()

        for side in range(2):

            @pl.when(has[side])
            def _():
                for kind in range(KINDS):
                    send_z(l, kind, side, za, own_piece(l, kind)).wait_send()

        def last_c(slot):
            for kind in range(KINDS):
                send_c(l, kind, slot).wait_send()

        loop(1, outer, last_z)
        loop(0, outer, last_y)
        others(last_c)


def on_device(mesh, *args):
    qn, qr, ku, vu, pool_lat, pool_rope, table, suf_lat, suf_rope, lengths = args
    layers, seqs, _ = qn.shape
    groups = mesh.shape["dp"]
    ring = mesh.shape["head"]
    heads_dev, rank = ku.shape[1], ku.shape[3]
    per, blk = pool_lat.shape[1], pool_lat.shape[2]
    suf = suf_lat.shape[2]
    nblk = table.shape[1]
    chunk = max(c for c in range(1, 7) if nblk % c == 0)
    rows_g = seqs * heads_dev
    rows = groups * rows_g
    slots = per * ring
    outer = ring // 2
    dims = (layers, seqs, groups, heads_dev, rank, blk, suf, per, ring, nblk, chunk)
    V = pltpu.VMEM
    D = pltpu.SemaphoreType.DMA
    scratch = [
        V(qr.shape, BF16), V(ku.shape, BF16), V(vu.shape, BF16), V(suf_lat.shape, BF16), V(suf_rope.shape, BF16),
        *[V((slots, blk, rank), BF16) for _ in range(layers)],
        *[V((slots, ROPE, blk), BF16) for _ in range(layers)],
        V((layers, groups, seqs, heads_dev * NOPE), BF16),
        V((layers, groups, seqs, heads_dev * ROPE), BF16),
        V((rank // 128, rows, 128), F32),
        V((layers, groups, rows_g, rank), BF16),
        V((layers, groups, rows_g, rank), BF16),
        V((rows, 128), F32),
        V((layers, rows, 128), BF16),
        V((layers, rows, 128), BF16),
        V((layers, rows, 1), F32),
        V((layers, rows, 1), F32),
        V((layers, rows, rank), F32),
        V((rows, chunk * blk), F32),
        V((chunk * blk, rank), BF16),
        V((ROPE, chunk * blk), BF16),
        V((layers, groups, rows_g, rank), BF16),
        V((layers, groups, rows_g, rank), BF16),
        V((layers, groups, 8, 128), F32),
        V((layers, groups, 8, 128), F32),
        V((layers, groups, seqs, heads_dev * VDIM), BF16),
        D((5, layers)), D((2, layers)), D((3, layers)),
        *[D((layers, groups)) for _ in range(12)],
        D((layers, KINDS, 2, outer)),
        *[D((layers, KINDS, outer)) for _ in range(3)],
        *[D((layers, KINDS, ring)) for _ in range(2)],
    ]
    hbm = pl.BlockSpec(memory_space=pl.ANY)
    smem = pl.BlockSpec(memory_space=pltpu.SMEM)
    return pl.pallas_call(
        functools.partial(kernel, dims),
        out_shape=jax.ShapeDtypeStruct((layers, seqs, HEADS * VDIM), BF16),
        in_specs=[hbm] * 6 + [smem] + [hbm] * 2 + [smem],
        out_specs=hbm,
        scratch_shapes=scratch,
        compiler_params=pltpu.CompilerParams(
            collective_id=0, has_side_effects=True, vmem_limit_bytes=60 * 1024 * 1024
        ),
        name="latent_attention",
    )(*args)


def solution(mesh):
    return jax.shard_map(
        functools.partial(on_device, mesh),
        mesh=mesh,
        in_specs=(
            P(None, ("dp", "head"), None),
            P(None, ("dp", "head"), None),
            P(None, "dp", None, None),
            P(None, "dp", None, None),
            P(None, "head", None, None),
            P(None, "head", None, None),
            P(),
            P(None, ("dp", "head"), None, None),
            P(None, ("dp", "head"), None, None),
            P(("dp", "head")),
        ),
        out_specs=P(None, ("dp", "head"), None),
        check_vma=False,
    )
```
